512 devices in a mesh: wide: 32 (over y, z_hi), narrow: 16 (over z_lo, x, core).
Axes of the slice: x: 4, y: 8, z: 8 (z_hi: 4, z_lo: 2; z = z_hi * 2 + z_lo), core: 2. Of those that a mesh axis runs over, the one named last changes fastest.
Arguments:
- daily_fields: bfloat16 [1024, 704, 1440], P('narrow', 'wide'), may hold values from -6 to 6
- order_table: int32 [384], replicated, may hold values from 0 to 383, as said below
- lag_days: int32 [3], replicated, may hold values from 1 to 8, as said below
- lag_weights: float32 [3, 384, 384, 2], P(None, 'narrow', 'wide'), may hold values from -0.5 to 0.5
Outputs:
- noise_variance: float32 [384, 384, 2], P('narrow', 'wide')
- covariance_panel: float32 [384, 48, 6144], P('wide', None, 'narrow')
The draws below stay inside these ranges and needn't reach their ends.
Inputs may be any that keep to these rules, and one draw needn't show every extreme that they name: `order_table`: slots 2k and 2k+1 hold the two orders m and 383 - m of one pair, the even one in slot 2k; every order appears once. `lag_days`: three different lags; one of them is 8.
All inputs are finite; a program needn't handle non-finite values.
Results may differ from the reference program's by a relative error of at most 0.0087.
Values may be sent and summed in bfloat16 or wider, within the bound.
A program may use at most 64 MiB of HBM per device.

```python
import math
import jax
import jax.numpy as jnp
from jax import lax

NLAT = 704
NLON = 1440
M = 384
L = 384
T_DEV = 64
LAGMAX = 8
ROW_DEG = 3
TIMES = 1024
DEG_DEV = 24
N_NARROW = 16


def draw_order_table(key, part):
    pair_order = jax.random.permutation(jax.random.fold_in(key, 11), M // 2).astype(jnp.int32)
    partner = M - 1 - pair_order
    even_member = jnp.where(pair_order % 2 == 0, pair_order, partner)
    odd_member = jnp.where(pair_order % 2 == 0, partner, pair_order)
    return jnp.stack([even_member, odd_member], axis=1).reshape(M).astype(jnp.int32)


def draw_lag_days(key, part):
    shorter = jax.random.permutation(jax.random.fold_in(key, 13), LAGMAX - 1)[:2].astype(jnp.int32) + 1
    picked = jnp.concatenate([shorter, jnp.array([LAGMAX], dtype=jnp.int32)])
    arrangement = jax.random.permutation(jax.random.fold_in(key, 17), 3)
    return picked[arrangement].astype(jnp.int32)


def steps_of(rng, shape, shards, low, high):
    def one(axis_at, blocks):
        heights = jax.random.uniform(jax.random.fold_in(jax.random.fold_in(rng, 6), axis_at), (blocks,), jnp.float32, low / len(shards), high / len(shards))
        return jnp.repeat(jnp.exp(heights), shape[axis_at] // blocks).reshape((-1,) + (1,) * (len(shape) - axis_at - 1))

    gain = one(*shards[0])
    for cut in shards[1:]:
        gain = gain * one(*cut)
    return gain


def normal_values(key, extent, deviation, limit, split=(), kind=jnp.bfloat16):
    result = jax.random.normal(key, extent, jnp.float32) * deviation
    if len(split) > 0:
        result = steps_of(key, extent, split, -0.22, 0.18) * result
    return jnp.clip(result, min=-limit, max=limit).astype(kind)


def setup_inputs(seed: int = 0) -> dict:
    splits = jax.random.split(jax.random.key(seed), 5)
    daily_fields = normal_values(splits[0], (TIMES, NLAT, NLON), 1.0, 6.0, ((0, 16), (1, 32)))
    order_table = draw_order_table(jax.random.fold_in(splits[4], 71), 0)
    lag_days = draw_lag_days(jax.random.fold_in(splits[4], 71), 0)
    lag_weights = jnp.clip(jax.random.uniform(splits[3], (3, L, M, 2), jnp.float32, -0.5, 0.5) * steps_of(splits[3], (3, L, M, 2), ((1, 16), (2, 32)), -0.4, 0.0), -0.5, 0.5)
    return dict(daily_fields=daily_fields, order_table=order_table, lag_days=lag_days, lag_weights=lag_weights)


def dft_table(order_table):
    longitude = jnp.arange(NLON, dtype=jnp.int32)
    phase_turns = order_table.astype(jnp.int32)[:, None] * longitude[None, :] % NLON
    angle = phase_turns.astype(jnp.float32) * (2.0 * math.pi / NLON)
    norm_scale = 1.0 / math.sqrt(NLON)
    return jnp.stack([jnp.cos(angle) * norm_scale, -jnp.sin(angle) * norm_scale], axis=1).astype(jnp.bfloat16)

def lat_basis():
    degree = jnp.arange(L, dtype=jnp.int32)
    odd_lat = 2 * jnp.arange(NLAT, dtype=jnp.int32) + 1
    period = 4 * NLAT
    even_turns = degree[:, None] * odd_lat[None, :] % period
    odd_turns = (degree[:, None] + 1) * odd_lat[None, :] % period
    angle_unit = math.pi / (2 * NLAT)
    norm_scale = math.sqrt(2.0 / NLAT)
    cosines = jnp.cos(even_turns.astype(jnp.float32) * angle_unit) * norm_scale
    sines = jnp.sin(odd_turns.astype(jnp.float32) * angle_unit) * norm_scale
    return jnp.stack([cosines, sines]).astype(jnp.bfloat16)

def reference(daily_fields, order_table, lag_days, lag_weights):
    dft_rows = dft_table(order_table).reshape(M * 2, NLON)
    lat_table = lat_basis()
    slot_basis = lat_table[order_table % 2].astype(jnp.float32)
    blocks = daily_fields.reshape(TIMES // T_DEV, T_DEV, NLAT, NLON)

    def transform(day_block):
        spectra = jnp.dot(day_block.reshape(T_DEV * NLAT, NLON), dft_rows.T, preferred_element_type=jnp.float32)
        spectra = spectra.astype(jnp.bfloat16).reshape(T_DEV, NLAT, M, 2)
        coeffs = jnp.einsum('slj,tjsc->lsct', slot_basis, spectra.astype(jnp.float32))
        return coeffs.astype(jnp.bfloat16)
    coeffs = lax.map(transform, blocks)
    coeffs = jnp.moveaxis(coeffs, 0, 3).reshape(L, M, 2, TIMES)
    day_index = jnp.arange(TIMES, dtype=jnp.int32)

    def degree_rows(inputs):
        series, weights = inputs
        series32 = series.astype(jnp.float32)
        residual = series32
        for position in range(3):
            shifted = jnp.roll(series32, lag_days[position], axis=-1)
            residual = residual - weights[position][..., None] * shifted
        residual = jnp.where(day_index >= LAGMAX, residual, 0.0)
        spread = lax.optimization_barrier(jnp.sum(residual * residual, axis=-1)) / (TIMES - LAGMAX)
        return (spread, residual[:, 0, :].astype(jnp.bfloat16))
    noise_variance, real_rows = lax.map(degree_rows, (coeffs, jnp.moveaxis(lag_weights, 0, 1)))
    pick_index = jnp.arange(ROW_DEG * N_NARROW, dtype=jnp.int32)
    row_degrees = pick_index // ROW_DEG * DEG_DEV + pick_index % ROW_DEG
    col_degrees = jnp.arange(N_NARROW, dtype=jnp.int32) * DEG_DEV + ROW_DEG
    row_series = real_rows[row_degrees].astype(jnp.float32)
    column_series = real_rows[col_degrees].astype(jnp.float32)
    cov_panel = jnp.einsum('jst,nqt->sjnq', row_series, column_series)
    cov_panel = cov_panel.reshape(M, ROW_DEG * N_NARROW, N_NARROW * M) / math.sqrt(TIMES - LAGMAX)
    return (noise_variance, cov_panel)
```

```python
import math

import jax
import jax.numpy as jnp
import numpy as np
from jax import lax
from jax.experimental import pallas as pl
from jax.experimental.pallas import tpu as pltpu
from jax.sharding import PartitionSpec as P

NLAT = 704
NLON = 1440
M = 384
L = 384
LAGMAX = 8
ROW_DEG = 3
WIDE = 32
NARROW = 16
CH = 3
SLOTS = 4
ROWS = 24
LANES = 128
PAIRS = NARROW // 2

BF16 = jnp.bfloat16
F32 = jnp.float32
MESH = pl.DeviceIdType.MESH

WIDE_OFFS = sorted(
    [(a, b) for a in range(8) for b in range(4) if (a, b) != (0, 0)],
    key=lambda p: (min(p[0], 8 - p[0]) + 2 * min(p[1], 4 - p[1]), p),
)
NARROW_OFFS = sorted(
    [(a, b, c) for a in range(2) for b in range(4) for c in range(2) if (a, b, c) != (0, 0, 0)],
    key=lambda p: (p[0] + min(p[1], 4 - p[1]), p),
)


def fourier_tables():
    order = np.arange(M)
    angle = (order[:, None] * np.arange(NLON)[None, :] % NLON) * (2.0 * math.pi / NLON)
    scale = 1.0 / math.sqrt(NLON)
    return np.stack([np.cos(angle) * scale, -np.sin(angle) * scale]).astype(np.float32)


def latitude_tables():
    degree = np.arange(L)
    odd = 2 * np.arange(NLAT) + 1
    unit = math.pi / (2 * NLAT)
    scale = math.sqrt(2.0 / NLAT)
    even_part = np.cos((degree[:, None] * odd[None, :] % (4 * NLAT)) * unit) * scale
    odd_part = np.sin(((degree[:, None] + 1) * odd[None, :] % (4 * NLAT)) * unit) * scale
    table = np.stack([even_part, odd_part]).reshape(2, L, WIDE, 11, 2)
    table = np.transpose(table, (0, 1, 2, 4, 3))
    table = np.pad(table, ((0, 0), (0, 0), (0, 0), (0, 0), (0, 1)))
    return table.reshape(2, L, WIDE * ROWS).astype(np.float32)


def wide_peer(me, off):
    y = lax.rem(lax.div(me, 4) + off[0], 8)
    z = lax.rem(lax.rem(me, 4) + off[1], 4)
    return y * 4 + z


def narrow_peer(me, off):
    z = lax.rem(lax.div(me, 8) + off[0], 2)
    x = lax.rem(lax.rem(lax.div(me, 2), 4) + off[1], 4)
    c = lax.rem(lax.rem(me, 2) + off[2], 2)
    return z * 8 + x * 2 + c


def kernel(
    order_ref, lag_ref, weight_ref, fourier_ref, lat_ref, x_ref,
    var_ref, panel_ref,
    table, wave, spec_out, spec_in, coef_out, coef_in, wexp, series,
    row_out, row_in, col_out, col_in, rows32, cols32, colmat,
    s_spec, r_spec, s_coef, r_coef, s_row, r_row, s_col, r_col, local,
):
    w = lax.axis_index("wide")
    n = lax.axis_index("narrow")

    barrier = pltpu.get_barrier_semaphore()
    for off in WIDE_OFFS:
        pl.semaphore_signal(barrier, inc=1, device_id={"wide": wide_peer(w, off)}, device_id_type=MESH)
    for off in NARROW_OFFS:
        pl.semaphore_signal(barrier, inc=1, device_id={"narrow": narrow_peer(n, off)}, device_id_type=MESH)

    def send_wide(source, target, ch, s_sem, r_sem):
        return [
            pltpu.make_async_remote_copy(
                src_ref=source(wide_peer(w, off)), dst_ref=target, send_sem=s_sem.at[ch, i],
                recv_sem=r_sem.at[ch, i], device_id={"wide": wide_peer(w, off)}, device_id_type=MESH,
            )
            for i, off in enumerate(WIDE_OFFS)
        ]

    def send_narrow(source, target, ch, s_sem, r_sem):
        return [
            pltpu.make_async_remote_copy(
                src_ref=source(narrow_peer(n, off)), dst_ref=target, send_sem=s_sem.at[ch, i],
                recv_sem=r_sem.at[ch, i], device_id={"narrow": narrow_peer(n, off)}, device_id_type=MESH,
            )
            for i, off in enumerate(NARROW_OFFS)
        ]

    def launch(copies):
        for copy in copies:
            copy.start()
        return copies

    def arrive(copies):
        copies[0].wait()
        for copy in copies[1:]:
            copy.wait_recv()

    def drain(copies):
        for copy in copies[1:]:
            copy.wait_send()

    lane128 = lax.broadcasted_iota(jnp.int32, (ROWS, LANES), 1)
    left = lane128 < 64
    pads = jnp.zeros((256, LANES), F32)
    for slot in (11, 23, 35):
        wave[pl.ds(slot * 256, 256), :] = pads

    spectra = []
    for ch in range(CH):
        hot = (
            order_ref[pl.ds(ch * 128, 128), :] == lax.broadcasted_iota(jnp.int32, (128, M), 1)
        ).astype(F32).astype(BF16)
        for c in range(2):
            table[pl.ds(c * 128, 128), :] = jnp.dot(
                hot, fourier_ref[c], preferred_element_type=F32
            ).astype(BF16)
        for at, count in ((0, 4), (4, 4), (8, 4), (12, 4), (16, 4), (20, 2)):
            days = x_ref[pl.ds(at, count)].reshape(count * 64, NLON)
            out = lax.dot_general(
                table[...], days, (((1,), (1,)), ((), ())), preferred_element_type=F32
            )
            for half in range(count // 2):
                piece = out[:, half * 128 : (half + 1) * 128]
                slot = at // 2 + half
                wave[pl.ds(slot * 256, 256), :] = piece
                wave[pl.ds((24 + slot) * 256, 256), :] = piece
                wave[pl.ds((12 + slot) * 256, 256), :] = pltpu.roll(piece, 64, 1)

        def regroup(d, carry, ch=ch):
            for q in range(SLOTS):
                real = wave[pl.ds(d * 4 + q, ROWS, stride=256), :]
                imag = wave[pl.ds(12 * 256 + 128 + d * 4 + q, ROWS, stride=256), :]
                blk = jnp.where(left, real, imag)
                rows32[pl.ds(q * ROWS, ROWS), :] = blk
            spec_out[ch, d] = rows32[pl.ds(0, SLOTS * ROWS), :].astype(BF16)
            return carry

        lax.fori_loop(0, WIDE, regroup, 0)
        if ch == 0:
            pl.semaphore_wait(barrier, len(WIDE_OFFS) + len(NARROW_OFFS))
        spectra.append(
            launch(send_wide(lambda d, ch=ch: spec_out.at[ch, d], spec_in.at[ch, w], ch, s_spec, r_spec))
        )
        own = pltpu.make_async_copy(spec_out.at[ch, w], spec_in.at[ch, w], local.at[0, ch])
        own.start()
        spectra[-1].insert(0, own)

    coefs, row_copies, col_copies = [], [], []
    variance = jnp.zeros((2 * ROWS, LANES), F32)
    lane48 = lax.broadcasted_iota(jnp.int32, (2 * ROWS, LANES), 1)
    day = lax.rem(lane48, 64)
    left48 = lane48 < 64

    def latitude(ch):
        arrive(spectra[ch])
        parts = []
        for e in range(2):
            columns = []
            for q2 in range(2):
                at = (2 * q2 + e) * ROWS
                blk = spec_in[ch].astype(F32)[:, at : at + ROWS, :]
                columns.append(blk.reshape(WIDE * ROWS, LANES).astype(BF16))
            right = jnp.concatenate(columns, axis=1)
            parts.append(jnp.dot(lat_ref[e], right, preferred_element_type=F32))
        for m in range(NARROW):
            both = jnp.concatenate([parts[0][m * 24 : m * 24 + 24], parts[1][m * 24 : m * 24 + 24]], axis=0)
            coef_out[ch, m] = both.astype(BF16)
        copies = launch(
            send_narrow(lambda m: coef_out.at[ch, m], coef_in.at[ch, n], ch, s_coef, r_coef)
        )
        own = pltpu.make_async_copy(coef_out.at[ch, n], coef_in.at[ch, n], local.at[1, ch])
        own.start()
        copies.insert(0, own)
        coefs.append(copies)

    def residuals(ch, variance):
        arrive(coefs[ch])
        for q2 in range(2):
            k = 2 * ch + q2
            for i in range(3):
                re = jnp.broadcast_to(weight_ref[i, :, 2 * k : 2 * k + 1], (2 * ROWS, LANES))
                im = jnp.broadcast_to(weight_ref[i, :, 2 * k + 1 : 2 * k + 2], (2 * ROWS, LANES))
                wexp[i] = jnp.where(left48, re, im)
            before = jnp.zeros((2 * ROWS, LANES), F32)
            total = jnp.zeros((2 * ROWS, LANES), F32)
            held = None
            for m in range(NARROW):
                now = coef_in[ch, m, :, q2 * LANES : (q2 + 1) * LANES].astype(F32)
                res = now
                for i in range(3):
                    lag = lag_ref[i]
                    mixed = jnp.where(day >= 64 - lag, before, now)
                    res = res - wexp[i] * pltpu.roll(mixed, lag, 1)
                if m == 0:
                    res = jnp.where(day >= LAGMAX, res, 0.0)
                total = total + res * res
                before = pltpu.roll(now, 64, 1)
                for e in range(2):
                    top = res[e * ROWS : e * ROWS + 8]
                    if m % 2 == 0:
                        held = (held or []) + [top] if e == 1 else [top]
                    else:
                        both = jnp.where(left[:8], held[e], pltpu.roll(top, 64, 1))
                        series[pl.ds((2 * q2 + e) * 64 + (m // 2) * 8, 8), :] = both
            re = jnp.sum(jnp.where(left48, total, 0.0), axis=1, keepdims=True)
            im = jnp.sum(jnp.where(left48, 0.0, total), axis=1, keepdims=True)
            variance = variance + jnp.where(lane48 == 2 * k, re, 0.0) + jnp.where(lane48 == 2 * k + 1, im, 0.0)
        parts = []
        for q in range(SLOTS):
            for l in range(ROW_DEG):
                parts.append(series[pl.ds(q * 64 + l, PAIRS, stride=8), :])
        row_out[ch] = jnp.concatenate(parts, axis=0).astype(BF16)
        parts = [series[pl.ds(q * 64 + ROW_DEG, PAIRS, stride=8), :] for q in range(SLOTS)]
        col_out[ch] = jnp.concatenate(parts, axis=0).astype(BF16)
        copies = launch(send_wide(lambda d: col_out.at[ch], col_in.at[ch, w], ch, s_col, r_col))
        own = pltpu.make_async_copy(col_out.at[ch], col_in.at[ch, w], local.at[2, ch])
        own.start()
        copies.insert(0, own)
        col_copies.append(copies)
        copies = launch(send_narrow(lambda d: row_out.at[ch], row_in.at[ch, n], ch, s_row, r_row))
        own = pltpu.make_async_copy(row_out.at[ch], row_in.at[ch, n], local.at[3, ch])
        own.start()
        copies.insert(0, own)
        row_copies.append(copies)
        return variance

    latitude(0)
    latitude(1)
    variance = residuals(0, variance)
    latitude(2)
    variance = residuals(1, variance)
    variance = residuals(2, variance)
    var_ref[...] = variance / (NARROW * 64 - LAGMAX)

    for ch in range(CH):
        arrive(col_copies[ch])
        for d in range(WIDE):
            cols32[pl.ds((d * 12 + ch * 4) * 8, 32), :] = col_in[ch, d].astype(F32)
    for p in range(PAIRS):
        colmat[:, p * LANES : (p + 1) * LANES] = cols32[pl.ds(p, M, stride=8), :].astype(BF16)
    for ch in range(CH):
        arrive(row_copies[ch])
        for m in range(NARROW):
            blk = row_in[ch, m].astype(F32)
            for q in range(SLOTS):
                rows32[pl.ds(q * 384 + m * 24, 24), :] = blk[q * 24 : q * 24 + 24]
        for q in range(SLOTS):
            pieces = [rows32[pl.ds(q * 384 + p, 48, stride=8), :] for p in range(PAIRS)]
            rows = jnp.concatenate(pieces, axis=1).astype(BF16)
            out = lax.dot_general(
                rows, colmat[...], (((1,), (1,)), ((), ())), preferred_element_type=F32
            )
            panel_ref[ch * SLOTS + q] = out / math.sqrt(NARROW * 64 - LAGMAX)

    for copies in spectra + coefs + row_copies + col_copies:
        drain(copies)


def body(daily_fields, order_table, lag_days, lag_weights):
    fourier = jnp.asarray(fourier_tables(), BF16)
    lat = jnp.asarray(latitude_tables(), BF16)
    x = jnp.transpose(daily_fields, (1, 0, 2))
    order = jnp.transpose(order_table.reshape(WIDE, CH, SLOTS), (1, 0, 2)).reshape(M, 1)
    weights = jnp.transpose(lag_weights.reshape(3, 24, 6, 2, 2), (0, 3, 1, 2, 4)).reshape(3, 48, 12)
    vmem = pl.BlockSpec(memory_space=pltpu.VMEM)
    dma = pltpu.SemaphoreType.DMA
    nw, nn = len(WIDE_OFFS), len(NARROW_OFFS)
    variance, panel = pl.pallas_call(
        kernel,
        out_shape=(
            jax.ShapeDtypeStruct((2 * ROWS, LANES), F32),
            jax.ShapeDtypeStruct((CH * SLOTS, ROW_DEG * NARROW, M), F32),
        ),
        in_specs=[vmem, pl.BlockSpec(memory_space=pltpu.SMEM), vmem, vmem, vmem, vmem],
        out_specs=(vmem, vmem),
        scratch_shapes=[
            pltpu.VMEM((256, NLON), BF16),
            pltpu.VMEM((36 * 256, LANES), F32),
            pltpu.VMEM((CH, WIDE, SLOTS * ROWS, LANES), BF16),
            pltpu.VMEM((CH, WIDE, SLOTS * ROWS, LANES), BF16),
            pltpu.VMEM((CH, NARROW, 48, 256), BF16),
            pltpu.VMEM((CH, NARROW, 48, 256), BF16),
            pltpu.VMEM((3, 48, LANES), F32),
            pltpu.VMEM((SLOTS * 64, LANES), F32),
            pltpu.VMEM((CH, 96, LANES), BF16),
            pltpu.VMEM((CH, NARROW, 96, LANES), BF16),
            pltpu.VMEM((CH, 32, LANES), BF16),
            pltpu.VMEM((CH, WIDE, 32, LANES), BF16),
            pltpu.VMEM((SLOTS * 384, LANES), F32),
            pltpu.VMEM((M * 8, LANES), F32),
            pltpu.VMEM((M, PAIRS * LANES), BF16),
            dma((CH, nw)), dma((CH, nw)), dma((CH, nn)), dma((CH, nn)),
            dma((CH, nn)), dma((CH, nn)), dma((CH, nw)), dma((CH, nw)), dma((4, CH)),
        ],
        compiler_params=pltpu.CompilerParams(
            collective_id=0, has_side_effects=True, vmem_limit_bytes=60 * 1024 * 1024
        ),
        name="sphere",
    )(order, lag_days, weights, fourier, lat, x)
    noise = jnp.transpose(variance[:, :12].reshape(2, 24, 6, 2), (1, 2, 0, 3)).reshape(24, 12, 2)
    return noise, panel


def solution(mesh):
    placed = (P("narrow", "wide", None), P(), P(), P(None, "narrow", "wide", None))
    return jax.shard_map(
        body,
        mesh=mesh,
        in_specs=placed,
        out_specs=(P("narrow", "wide", None), P("wide", None, "narrow")),
        check_vma=False,
    )
```

```python
import math

import jax
import jax.numpy as jnp
import numpy as np
from jax import lax
from jax.experimental import pallas as pl
from jax.experimental.pallas import tpu as pltpu
from jax.sharding import PartitionSpec as P

NLAT = 704
NLON = 1440
M = 384
L = 384
LAGMAX = 8
ROW_DEG = 3
WIDE = 32
NARROW = 16
CH = 6
AHEAD = 2
ROWS = 24
LANES = 128
PAIRS = NARROW // 2
BAND = 2 * WIDE * 2

BF16 = jnp.bfloat16
F32 = jnp.float32
MESH = pl.DeviceIdType.MESH

Z_OFFS = [(0, 1), (0, 3), (0, 2)]
Y_OFFS = [(1, 0), (7, 0), (2, 0), (6, 0), (3, 0), (5, 0), (4, 0)]
ZLO_OFFS = [(1, 0, 0)]
XC_OFFS = [(0, 0, 1), (0, 1, 0), (0, 3, 0), (0, 1, 1), (0, 3, 1), (0, 2, 0), (0, 2, 1)]


def fourier_tables():
    order = np.arange(M)
    angle = (order[:, None] * np.arange(NLON)[None, :] % NLON) * (2.0 * math.pi / NLON)
    scale = 1.0 / math.sqrt(NLON)
    return np.stack([np.cos(angle) * scale, -np.sin(angle) * scale]).astype(np.float32)


def latitude_tables():
    degree = np.arange(L)
    odd = 2 * np.arange(NLAT) + 1
    unit = math.pi / (2 * NLAT)
    scale = math.sqrt(2.0 / NLAT)
    even_part = np.cos((degree[:, None] * odd[None, :] % (4 * NLAT)) * unit) * scale
    odd_part = np.sin(((degree[:, None] + 1) * odd[None, :] % (4 * NLAT)) * unit) * scale
    table = np.stack([even_part, odd_part]).reshape(2, L, WIDE, 11, 2)
    table = np.transpose(table, (0, 1, 2, 4, 3))
    table = np.pad(table, ((0, 0), (0, 0), (0, 0), (0, 0), (0, 1)))
    return table.reshape(2, L, WIDE * ROWS).astype(np.float32)


def wide_peer(me, off):
    y = lax.rem(lax.div(me, 4) + off[0], 8)
    z = lax.rem(lax.rem(me, 4) + off[1], 4)
    return y * 4 + z


def narrow_peer(me, off):
    z = lax.rem(lax.div(me, 8) + off[0], 2)
    x = lax.rem(lax.rem(lax.div(me, 2), 4) + off[1], 4)
    c = lax.rem(lax.rem(me, 2) + off[2], 2)
    return z * 8 + x * 2 + c


def wide_step(me, k):
    j = lax.div(k, 4)
    up = lax.div(j + 1, 2)
    dy = lax.rem(lax.rem(j, 2) * up + (1 - lax.rem(j, 2)) * (8 - up), 8)
    h = lax.rem(k, 4)
    dz = (h + 1 - lax.rem(h, 2)) * lax.div(h + 3, 4) * (1 - lax.div(h, 3)) + 2 * lax.div(h, 3)
    return wide_peer(me, (dy, dz))


def narrow_step(me, k):
    h = lax.div(k, 4)
    dx = (h + 1 - lax.rem(h, 2)) * lax.div(h + 3, 4) * (1 - lax.div(h, 3)) + 2 * lax.div(h, 3)
    return narrow_peer(me, (lax.rem(k, 2), dx, lax.rem(lax.div(k, 2), 2)))


def each(start, stop, act):
    def step(k, carry):
        act(k)
        return carry

    lax.fori_loop(start, stop, step, 0)


def kernel(
    order_ref, lag_ref, weight_ref, fourier_ref, lat_ref, x_ref,
    var_ref, panel_ref,
    table, wave, spec_out, spec_in, coef_out, coef_in, wexp, series,
    row_out, row_in, col_out, col_in, rows32, cols32, colmat,
    s_spec, r_spec, s_coef, r_coef, s_row, r_row, s_col, r_col, local,
):
    w = lax.axis_index("wide")
    n = lax.axis_index("narrow")
    row_at = 2 * lax.rem(n, 8) + lax.div(n, 8)

    barrier = pltpu.get_barrier_semaphore()
    each(1, WIDE, lambda k: pl.semaphore_signal(
        barrier, inc=1, device_id={"wide": wide_step(w, k)}, device_id_type=MESH))
    each(1, NARROW, lambda k: pl.semaphore_signal(
        barrier, inc=1, device_id={"narrow": narrow_step(n, k)}, device_id_type=MESH))

    def spectrum(ch, k):
        d = wide_step(w, k)
        return pltpu.make_async_remote_copy(
            src_ref=spec_out.at[ch, d], dst_ref=spec_in.at[ch, w], send_sem=s_spec.at[ch, k - 1],
            recv_sem=r_spec.at[ch, k - 1], device_id={"wide": d}, device_id_type=MESH,
        )

    def coefficient(ch, k):
        d = narrow_step(n, k)
        return pltpu.make_async_remote_copy(
            src_ref=coef_out.at[ch, d], dst_ref=coef_in.at[ch, n], send_sem=s_coef.at[ch, k - 1],
            recv_sem=r_coef.at[ch, k - 1], device_id={"narrow": d}, device_id_type=MESH,
        )

    def to_wide(offs, source, target, ch, at):
        return [
            pltpu.make_async_remote_copy(
                src_ref=source, dst_ref=target, send_sem=s_col.at[ch, at + i],
                recv_sem=r_col.at[ch, at + i], device_id={"wide": wide_peer(w, off)}, device_id_type=MESH,
            )
            for i, off in enumerate(offs)
        ]

    def to_narrow(offs, source, target, ch, at):
        return [
            pltpu.make_async_remote_copy(
                src_ref=source, dst_ref=target, send_sem=s_row.at[ch, at + i],
                recv_sem=r_row.at[ch, at + i], device_id={"narrow": narrow_peer(n, off)}, device_id_type=MESH,
            )
            for i, off in enumerate(offs)
        ]

    def own_spec(ch):
        return pltpu.make_async_copy(spec_out.at[ch, w], spec_in.at[ch, w], local.at[0, ch])

    def own_coef(ch):
        return pltpu.make_async_copy(coef_out.at[ch, n], coef_in.at[ch, n], local.at[1, ch])

    def own_col(ch):
        return pltpu.make_async_copy(col_out.at[ch], col_in.at[ch, w], local.at[2, ch])

    def own_row(ch):
        return pltpu.make_async_copy(row_out.at[ch], row_in.at[ch, row_at], local.at[3, ch])

    def col_near(ch):
        return to_wide(Z_OFFS, col_out.at[ch], col_in.at[ch, w], ch, 0)

    def row_near(ch):
        return to_narrow(ZLO_OFFS, row_out.at[ch], row_in.at[ch, row_at], ch, 0)

    def col_far(ch):
        block = col_in.at[ch, pl.ds(pl.multiple_of(w - lax.rem(w, 4), 4), 4)]
        return to_wide(Y_OFFS, block, block, ch, len(Z_OFFS))

    def row_far(ch):
        block = row_in.at[ch, pl.ds(pl.multiple_of(2 * lax.rem(n, 8), 2), 2)]
        return to_narrow(XC_OFFS, block, block, ch, len(ZLO_OFFS))

    left = lax.broadcasted_iota(jnp.int32, (ROWS, LANES), 1) < 64
    lane48 = lax.broadcasted_iota(jnp.int32, (2 * ROWS, LANES), 1)
    day = lax.rem(lane48, 64)
    left48 = lane48 < 64

    for slot in (11, 23, 35):
        wave[pl.ds(slot * BAND, BAND), :] = jnp.zeros((BAND, LANES), F32)
    var_ref[...] = jnp.zeros((2 * ROWS, LANES), F32)

    def fourier(ch):
        half = BAND // 2
        mine = order_ref[pl.ds(pl.multiple_of(ch * half, half), half), :]
        hot = (mine == lax.broadcasted_iota(jnp.int32, (half, M), 1)).astype(F32).astype(BF16)
        for c in range(2):
            table[c * half : (c + 1) * half, :] = jnp.dot(
                hot, fourier_ref[c], preferred_element_type=F32
            ).astype(BF16)
        for at, count in ((0, 4), (4, 4), (8, 4), (12, 4), (16, 4), (20, 2)):
            days = x_ref[pl.ds(at, count)].reshape(count * 64, NLON)
            out = lax.dot_general(
                table[...], days, (((1,), (1,)), ((), ())), preferred_element_type=F32
            )
            for i in range(count // 2):
                piece = out[:, i * LANES : (i + 1) * LANES]
                slot = at // 2 + i
                wave[pl.ds(slot * BAND, BAND), :] = piece
                wave[pl.ds((24 + slot) * BAND, BAND), :] = piece
                wave[pl.ds((12 + slot) * BAND, BAND), :] = pltpu.roll(piece, 64, 1)

        def regroup(d):
            blocks = []
            for q in range(2):
                real = wave[pl.ds(d * 2 + q, ROWS, stride=BAND), :]
                imag = wave[pl.ds(12 * BAND + half + d * 2 + q, ROWS, stride=BAND), :]
                blocks.append(jnp.where(left, real, imag))
            spec_out[ch, d] = jnp.concatenate(blocks, axis=0).astype(BF16)

        each(0, WIDE, regroup)

    def send_spectra(ch):
        each(1, WIDE, lambda k: spectrum(ch, k).start())
        own_spec(ch).start()

    def latitude(ch):
        own_spec(ch).wait()
        each(1, WIDE, lambda k: spectrum(ch, k).wait_recv())
        got = spec_in[ch].astype(F32)
        parts = []
        for e in range(2):
            right = got[:, e * ROWS : (e + 1) * ROWS, :].reshape(WIDE * ROWS, LANES).astype(BF16)
            parts.append(jnp.dot(lat_ref[e], right, preferred_element_type=F32))
        for m in range(NARROW):
            both = jnp.concatenate([p[m * ROWS : (m + 1) * ROWS] for p in parts], axis=0)
            coef_out[ch, m] = both.astype(BF16)
        each(1, NARROW, lambda k: coefficient(ch, k).start())
        own_coef(ch).start()

    def residuals(ch):
        own_coef(ch).wait()
        each(1, NARROW, lambda k: coefficient(ch, k).wait_recv())
        lane12 = lax.broadcasted_iota(jnp.int32, (2 * ROWS, 12), 1)
        for i in range(3):
            re = jnp.sum(jnp.where(lane12 == 2 * ch, weight_ref[i], 0.0), axis=1, keepdims=True)
            im = jnp.sum(jnp.where(lane12 == 2 * ch + 1, weight_ref[i], 0.0), axis=1, keepdims=True)
            wexp[i] = jnp.where(left48, re, im)
        before = jnp.zeros((2 * ROWS, LANES), F32)
        total = jnp.zeros((2 * ROWS, LANES), F32)
        held = [None, None]
        for m in range(NARROW):
            now = coef_in[ch, m].astype(F32)
            res = now
            for i in range(3):
                lag = lag_ref[i]
                mixed = jnp.where(day >= 64 - lag, before, now)
                res = res - wexp[i] * pltpu.roll(mixed, lag, 1)
            if m == 0:
                res = jnp.where(day >= LAGMAX, res, 0.0)
            total = total + res * res
            before = pltpu.roll(now, 64, 1)
            for e in range(2):
                top = res[e * ROWS : e * ROWS + 8]
                if m % 2 == 0:
                    held[e] = top
                else:
                    both = jnp.where(left[:8], held[e], pltpu.roll(top, 64, 1))
                    series[pl.ds(e * 64 + (m // 2) * 8, 8), :] = both
        re = jnp.sum(jnp.where(left48, total, 0.0), axis=1, keepdims=True)
        im = jnp.sum(jnp.where(left48, 0.0, total), axis=1, keepdims=True)
        var_ref[...] += jnp.where(lane48 == 2 * ch, re, 0.0) + jnp.where(lane48 == 2 * ch + 1, im, 0.0)
        pieces = [
            series[pl.ds(e * 64 + l, PAIRS, stride=8), :] for e in range(2) for l in range(ROW_DEG)
        ]
        row_out[ch] = jnp.concatenate(pieces, axis=0).astype(BF16)
        pieces = [series[pl.ds(e * 64 + ROW_DEG, PAIRS, stride=8), :] for e in range(2)]
        col_out[ch] = jnp.concatenate(pieces, axis=0).astype(BF16)
        for copy in [own_col(ch), own_row(ch)] + col_near(ch) + row_near(ch):
            copy.start()

    def spread(ch):
        own_col(ch).wait()
        for copy in col_near(ch):
            copy.wait_recv()
        for copy in col_far(ch):
            copy.start()
        own_row(ch).wait()
        for copy in row_near(ch):
            copy.wait_recv()
        for copy in row_far(ch):
            copy.start()

    def within(step, behind, act):
        ch = step - behind

        @pl.when((ch >= 0) & (ch < CH))
        def _():
            act(ch)

    def stage(step):
        within(step, 0, fourier)

        @pl.when(step == 0)
        def _():
            pl.semaphore_wait(barrier, WIDE + NARROW - 2)

        within(step, AHEAD, latitude)
        within(step, 0, send_spectra)
        within(step, AHEAD + 1, residuals)
        within(step, AHEAD + 2, spread)

    each(0, CH + AHEAD + 2, stage)

    def columns(ch):
        for copy in col_far(ch):
            copy.wait_recv()
        for d in range(WIDE):
            cols32[pl.ds(pl.multiple_of((d * 12 + ch * 2) * 8, 8), 16), :] = col_in[ch, d].astype(F32)

    each(0, CH, columns)
    for p in range(PAIRS):
        colmat[:, p * LANES : (p + 1) * LANES] = cols32[pl.ds(p, M, stride=8), :].astype(BF16)

    def panel(ch):
        for copy in row_far(ch):
            copy.wait_recv()
        for m in range(NARROW):
            blk = row_in[ch, 2 * (m % 8) + m // 8].astype(F32)
            for q in range(2):
                rows32[pl.ds(q * 384 + m * 24, 24), :] = blk[q * 24 : q * 24 + 24]
        rows = jnp.concatenate(
            [
                jnp.concatenate([rows32[pl.ds(q * 384 + p, 48, stride=8), :] for p in range(PAIRS)], axis=1)
                for q in range(2)
            ],
            axis=0,
        ).astype(BF16)
        out = lax.dot_general(rows, colmat[...], (((1,), (1,)), ((), ())), preferred_element_type=F32)
        out = out / math.sqrt(NARROW * 64 - LAGMAX)
        for q in range(2):
            panel_ref[ch * 2 + q] = out[q * 48 : q * 48 + 48]

    each(0, CH, panel)
    var_ref[...] = var_ref[...] / (NARROW * 64 - LAGMAX)

    def drain(ch):
        each(1, WIDE, lambda k: spectrum(ch, k).wait_send())
        each(1, NARROW, lambda k: coefficient(ch, k).wait_send())
        for copy in col_near(ch) + col_far(ch) + row_near(ch) + row_far(ch):
            copy.wait_send()

    each(0, CH, drain)


def body(daily_fields, order_table, lag_days, lag_weights):
    fourier = jnp.asarray(fourier_tables(), BF16)
    lat = jnp.asarray(latitude_tables(), BF16)
    x = jnp.transpose(daily_fields, (1, 0, 2))
    order = jnp.transpose(order_table.reshape(WIDE, CH, 2), (1, 0, 2)).reshape(M, 1)
    weights = jnp.transpose(lag_weights.reshape(3, 24, 6, 2, 2), (0, 3, 1, 2, 4)).reshape(3, 48, 12)
    vmem = pl.BlockSpec(memory_space=pltpu.VMEM)
    dma = pltpu.SemaphoreType.DMA
    nw, nn = WIDE - 1, NARROW - 1
    nc, nr = len(Z_OFFS) + len(Y_OFFS), len(ZLO_OFFS) + len(XC_OFFS)
    variance, panel = pl.pallas_call(
        kernel,
        out_shape=(
            jax.ShapeDtypeStruct((2 * ROWS, LANES), F32),
            jax.ShapeDtypeStruct((CH * 2, ROW_DEG * NARROW, M), F32),
        ),
        in_specs=[vmem, pl.BlockSpec(memory_space=pltpu.SMEM), vmem, vmem, vmem, vmem],
        out_specs=(vmem, vmem),
        scratch_shapes=[
            pltpu.VMEM((BAND, NLON), BF16),
            pltpu.VMEM((36 * BAND, LANES), F32),
            pltpu.VMEM((CH, WIDE, 48, LANES), BF16),
            pltpu.VMEM((CH, WIDE, 48, LANES), BF16),
            pltpu.VMEM((CH, NARROW, 48, LANES), BF16),
            pltpu.VMEM((CH, NARROW, 48, LANES), BF16),
            pltpu.VMEM((3, 48, LANES), F32),
            pltpu.VMEM((2 * 64, LANES), F32),
            pltpu.VMEM((CH, 48, LANES), BF16),
            pltpu.VMEM((CH, NARROW, 48, LANES), BF16),
            pltpu.VMEM((CH, 16, LANES), BF16),
            pltpu.VMEM((CH, WIDE, 16, LANES), BF16),
            pltpu.VMEM((2 * 384, LANES), F32),
            pltpu.VMEM((M * 8, LANES), F32),
            pltpu.VMEM((M, PAIRS * LANES), BF16),
            dma((CH, nw)), dma((CH, nw)), dma((CH, nn)), dma((CH, nn)),
            dma((CH, nr)), dma((CH, nr)), dma((CH, nc)), dma((CH, nc)), dma((4, CH)),
        ],
        compiler_params=pltpu.CompilerParams(
            collective_id=0, has_side_effects=True, vmem_limit_bytes=60 * 1024 * 1024
        ),
        name="sphere",
    )(order, lag_days, weights, fourier, lat, x)
    noise = jnp.transpose(variance[:, :12].reshape(2, 24, 6, 2), (1, 2, 0, 3)).reshape(24, 12, 2)
    return noise, panel


def solution(mesh):
    placed = (P("narrow", "wide", None), P(), P(), P(None, "narrow", "wide", None))
    return jax.shard_map(
        body,
        mesh=mesh,
        in_specs=placed,
        out_specs=(P("narrow", "wide", None), P("wide", None, "narrow")),
        check_vma=False,
    )
```
